32 devices in a mesh: dp: 8 (over y, x, core), seq: 4 (over z).
Axes of the slice: x: 2, y: 2, z: 4, core: 2. Of those that a mesh axis runs over, the one named last changes fastest.
Arguments:
- block_input: bfloat16 [2, 8, 1024, 768], P(None, 'dp', 'seq'), may hold values from -6 to 6
- cotangent: bfloat16 [2, 8, 1024, 768], P(None, 'dp', 'seq'), may hold values from -6 to 6
- segments: int32 [2, 8, 1024], P(None, 'dp'), may hold values from 0 to 3, never falling along the last dimension, each value on 1 to 768 neighbouring positions
- rand_blocks: int32 [12, 16, 3], replicated, may hold values from 0 to 15
- w_attn: float32 [768, 2304], P('dp'), may hold values from -0.21875 to 0.21875
- w_out: float32 [768, 768], P('dp'), may hold values from -1.5 to 1.5
- w_up: float32 [768, 3072], P('dp'), may hold values from -0.21875 to 0.21875
- w_down: float32 [3072, 768], P('dp'), may hold values from -0.109375 to 0.109375
- up_bias: float32 [3072], P('dp'), may hold values from -3 to 3
- bias_rows: float32 [6, 768], P(None, 'dp'), may hold values from -2 to 2
- norm_gains: float32 [2, 768], P(None, 'dp'), may hold values from 0.25 to 1.75
Outputs:
- block_output: bfloat16 [2, 8, 1024, 768], P(None, 'dp', 'seq')
- input_grad: float32 [2, 8, 1024, 768], P(None, 'dp', 'seq')
- grad_w_attn: float32 [768, 2304], P('dp')
- grad_w_out: float32 [768, 768], P('dp')
- grad_w_up: float32 [768, 3072], P('dp')
- grad_w_down: float32 [3072, 768], P('dp')
- grad_up_bias: float32 [3072], P('dp')
- grad_bias_rows: float32 [6, 768], P(None, 'dp')
- grad_norm_gains: float32 [2, 768], P(None, 'dp')
The draws below stay inside these ranges and needn't reach their ends.
Inputs may be any that keep to these rules, and one draw needn't show every extreme that they name: `segments`: segment numbers never fall along a sequence. `rand_blocks`: block numbers within the sequence.
All inputs are finite; a program needn't handle non-finite values.
Results may differ from the reference program's by a relative error of at most 0.018.
Values may be sent and summed in bfloat16 or wider, within the bound.
No kernel may reach another device: no remote copies, remote signals or barrier semaphores. Data moves between devices by JAX's collectives and lax.ppermute only.
A program may use at most 192 MiB of HBM per device.

```python
import math
import jax
import jax.numpy as jnp
import numpy as np
from jax import lax

D = 768
HEADS = 12
FF = 3072
BLOCK = 64
RAND = 3
MB = 2
HEAD_DIM = 64
NB = 16
LEN = 1024
SEQB = 8


def place_ends(array, stream_key, least, largest):
    shape = array.shape
    spot = [jax.random.randint(jax.random.fold_in(stream_key, axis), (), 0, shape[axis]) for axis in range(len(shape))]
    array = array.at[tuple(spot)].set(least)
    longest = shape.index(max(shape))
    spot[longest] = (spot[longest] + 1) % shape[longest]
    return array.at[tuple(spot)].set(largest)


def levels(rng, extent, split, least, top_value):
    loudness = 1.0
    for axis_at, parts in split:
        draws = jax.random.uniform(jax.random.fold_in(jax.random.fold_in(rng, 6), axis_at), (parts,), jnp.float32, least / len(split), top_value / len(split))
        loudness = loudness * jnp.repeat(jnp.exp(draws), extent[axis_at] // parts).reshape((-1,) + (1,) * (len(extent) - 1 - axis_at))
    return loudness


def profile(count, total, limit, skew):
    portions = [(1 << 20) // math.isqrt(standing ** skew) + 1 for standing in range(2, count + 1)]
    rest, given = total - limit - (count - 1), [1] * (count - 1)
    while rest > 0:
        movable = [i for i in range(count - 1) if given[i] < limit]
        pool, remaining = sum([portions[i] for i in movable]), rest
        for i in movable:
            addition = min(limit - given[i], max(1, remaining * portions[i] // pool), rest)
            given[i] = given[i] + addition
            rest = rest - addition
    return np.array([limit] + given)


def uneven(rng, number_of, total, bound, slope):
    if number_of == 2:
        one = jax.random.randint(rng, (), max(1, total - bound), min(bound, total - 1) + 1)
        return jnp.stack([one, total - one])
    sizes = jnp.asarray(profile(number_of, total, bound, slope), jnp.int32)
    couples = (number_of - 1) // 2
    source_of, taker = sizes[1:1 + 2 * couples:2], sizes[2:2 + 2 * couples:2]
    margin = jnp.minimum(source_of - 1, bound - taker)
    shifted = jax.random.randint(jax.random.fold_in(rng, 1), (couples,), 0, 1 << 20) % (margin + 1)
    sizes = sizes.at[1:1 + 2 * couples:2].set(source_of - shifted).at[2:2 + 2 * couples:2].set(taker + shifted)
    return sizes[jax.random.permutation(jax.random.fold_in(rng, 2), number_of)]


def bell_draw(rng, shape, scale, most, split=(), held_as=jnp.bfloat16):
    array = scale * jax.random.normal(rng, shape, jnp.float32)
    if split:
        array = array * levels(rng, shape, split, -0.22, 0.18)
    return jnp.clip(array, -most, most).astype(held_as)


def setup_inputs(seed: int = 0) -> dict:
    key_of = jax.random.split(jax.random.key(seed), 12)
    block_input = bell_draw(key_of[0], (MB, SEQB, LEN, D), 1.0, 6.0, ((1, 8), (2, 4)))
    cotangent = bell_draw(key_of[1], (MB, SEQB, LEN, D), 1.0, 6.0, ((1, 8), (2, 4)))
    segments = jax.vmap(lambda own: jnp.searchsorted(jnp.cumsum(uneven(own, 4, LEN, 3 * LEN // 4, 1)), jnp.arange(LEN), side="right"))(jax.random.split(key_of[2], MB * SEQB)).reshape((MB, SEQB, LEN)).astype(jnp.int32)
    rand_blocks = place_ends(jax.random.randint(key_of[3], (HEADS, NB, RAND), 0, NB), jax.random.fold_in(key_of[3], 1), 0, NB - 1).astype(jnp.int32)
    w_attn = bell_draw(key_of[4], (D, 3 * D), D ** -0.5, 0.21875, ((0, 8),), jnp.float32)
    w_out = bell_draw(key_of[5], (D, D), (D // 64 + 4) ** -0.5, 1.5, ((0, 8),), jnp.float32)
    w_up = bell_draw(key_of[6], (D, FF), D ** -0.5, 0.21875, ((0, 8),), jnp.float32)
    w_down = bell_draw(key_of[7], (FF, D), FF ** -0.5, 0.109375, ((0, 8),), jnp.float32)
    up_bias = bell_draw(key_of[8], (FF,), 0.5, 3.0, ((0, 8),), jnp.float32)
    bias_rows = bell_draw(key_of[9], (6, D), 0.3, 2.0, ((1, 8),), jnp.float32)
    norm_gains = jnp.clip(1.0 + 0.15 * jax.random.normal(key_of[10], (2, D), jnp.float32), 0.25, 1.75)
    return dict(block_input=block_input, cotangent=cotangent, segments=segments, rand_blocks=rand_blocks, w_attn=w_attn, w_out=w_out, w_up=w_up, w_down=w_down, up_bias=up_bias, bias_rows=bias_rows, norm_gains=norm_gains)


EPSILON = 1e-05
MASKED = -1e+30

@jax.custom_vjp
def low(v):
    return lax.optimization_barrier(v.astype(jnp.bfloat16)).astype(jnp.float32)

@jax.custom_vjp
def low_back(v):
    return v

def low_keep(v):
    return (low(v), None)

def low_pass(kept, grad):
    return (grad,)

def back_keep(v):
    return (v, None)

def back_low(kept, grad):
    return (low(grad),)
low.defvjp(low_keep, low_pass)
low_back.defvjp(back_keep, back_low)

def layer_norm(tensor, gain_row, offset):
    centre = tensor - lax.optimization_barrier(jnp.mean(tensor, axis=-1, keepdims=True))
    spread = lax.optimization_barrier(jnp.mean(centre * centre, axis=-1, keepdims=True))
    return centre * lax.rsqrt(spread + EPSILON) * gain_row + offset

def visibility(rand_blocks):
    nblocks = LEN // BLOCK
    place = jnp.arange(LEN, dtype=jnp.int32) // BLOCK
    query_block = place[:, None]
    key_block = place[None, :]
    always = (query_block == 0) | (query_block == nblocks - 1) | (key_block == 0) | (key_block == nblocks - 1)
    always = always | (jnp.abs(query_block - key_block) <= 1)
    block_ids = jnp.arange(nblocks, dtype=jnp.int32)
    random_hit = jnp.any(rand_blocks[:, :, :, None] == block_ids[None, None, None, :], axis=2)
    random_hit = jnp.repeat(jnp.repeat(random_hit, BLOCK, axis=1), BLOCK, axis=2)
    return always[None] | random_hit

def sequence_forward(tokens, seg_ids, visible, params):
    w_attn, w_out, w_up, w_down, up_bias, bias_rows, norm_gains = params
    highest = lax.Precision.HIGHEST
    model_width = tokens.shape[1]
    projected = jnp.dot(tokens, w_attn, precision=highest)
    queries = low(low_back(projected[:, :model_width] + bias_rows[0]))
    keys_all = low(low_back(projected[:, model_width:2 * model_width]))
    values_all = low(low_back(projected[:, 2 * model_width:] + bias_rows[1]))
    query_heads = queries.reshape(LEN, HEADS, HEAD_DIM)
    key_heads = keys_all.reshape(LEN, HEADS, HEAD_DIM)
    value_heads = values_all.reshape(LEN, HEADS, HEAD_DIM)
    scores = jnp.einsum('qhd,khd->hqk', query_heads, key_heads, precision=highest) * HEAD_DIM ** (-0.5)
    scores = low_back(scores)
    allowed = visible & (seg_ids[:, None] == seg_ids[None, :])[None]
    scores = jnp.where(allowed, scores, MASKED)
    attn_probs = low(jax.nn.softmax(scores, axis=-1))
    mixture = jnp.einsum('hqk,khd->qhd', attn_probs, value_heads, precision=highest).reshape(LEN, model_width)
    attended = low(low_back(mixture))
    branch = low_back(jnp.dot(attended, w_out, precision=highest) + bias_rows[2])
    first_norm = layer_norm(tokens + branch, norm_gains[0], bias_rows[4])
    first_low = low(first_norm)
    pre_act = low_back(jnp.dot(first_low, w_up, precision=highest) + up_bias)
    activation = low(jax.nn.gelu(pre_act, approximate=False))
    ffn_out = low_back(jnp.dot(activation, w_down, precision=highest) + bias_rows[3])
    return layer_norm(first_norm + ffn_out, norm_gains[1], bias_rows[5])

def reference(block_input, cotangent, segments, rand_blocks, w_attn, w_out, w_up, w_down, up_bias, bias_rows, norm_gains):
    visible = visibility(rand_blocks)
    tokens = block_input.astype(jnp.float32).reshape(-1, LEN, D)
    seg_rows = segments.reshape(-1, LEN)
    params = (w_attn, w_out, w_up, w_down, up_bias, bias_rows, norm_gains)

    def seq_step(paired, rounded):
        return sequence_forward(paired[0], paired[1], visible, rounded)
    checked = jax.checkpoint(seq_step)

    def forward(tokens, params):
        rounded = tuple((low(member) for member in params))
        return lax.map(lambda paired: checked(paired, rounded), (tokens, seg_rows))
    outputs, pullback = jax.vjp(forward, tokens, params)
    input_grad, gradients = pullback(cotangent.astype(jnp.float32).reshape(outputs.shape))
    block_output = outputs.reshape(block_input.shape).astype(jnp.bfloat16)
    return (block_output, input_grad.reshape(block_input.shape), gradients[0], gradients[1], gradients[2], gradients[3], gradients[4], gradients[5], gradients[6])
```

```python
import jax
import jax.numpy as jnp
from jax import lax
from jax.sharding import PartitionSpec as P

EPSILON = 1e-05
MASKED = -1e30
GROUP = 8
BOTH = ("dp", "seq")
F32 = jnp.float32
BF16 = jnp.bfloat16


def layer_norm(tensor, gain_row, offset):
    centre = tensor - jnp.mean(tensor, axis=-1, keepdims=True)
    spread = jnp.mean(centre * centre, axis=-1, keepdims=True)
    return centre * lax.rsqrt(spread + EPSILON) * gain_row + offset


def gelu_exact(tensor):
    return jax.nn.gelu(tensor, approximate=False)


def col_sums(tensor):
    return jnp.sum(tensor.astype(F32), axis=0)


def outer_grad(left, right):
    return lax.dot_general(left, right, (((0,), (0,)), ((), ())), preferred_element_type=F32)


def times_transposed(left, right):
    return lax.dot_general(left, right, (((1,), (1,)), ((), ())), preferred_element_type=F32)


def swap(value, axis, bit):
    size = lax.axis_size(axis)
    return lax.ppermute(value, axis, [(i, i ^ bit) for i in range(size)])


def gather_chunks(mine):
    rows = mine.shape[0]
    half = rows // 32 * 16
    first = swap(mine, "dp", 2)
    second = swap(mine, "dp", 4)
    low = swap(first[:half], "dp", 4)
    high = swap(second[half:], "dp", 2)
    even = jnp.stack([mine, first, second, jnp.concatenate([low, high])])
    odd = swap(even, "dp", 1)
    full = jnp.stack([even, odd], axis=1).reshape((GROUP,) + mine.shape)
    bit = GROUP
    while bit < lax.axis_size("dp"):
        full = jnp.concatenate([full, swap(full, "dp", bit)])
        bit *= 2
    return full


def by_owner(chunks):
    own = lax.axis_index("dp")
    return jnp.stack(
        [lax.dynamic_index_in_dim(chunks, own ^ k, 0, False) for k in range(chunks.shape[0])]
    )


def reduce_chunks(chunks):
    bit = chunks.shape[0] // 2
    while bit >= GROUP:
        other = swap(chunks[bit:].astype(BF16), "dp", bit)
        chunks = chunks[:bit] + other.astype(F32)
        bit //= 2
    rows = chunks.shape[1]
    half = rows // 32 * 16
    pairs = chunks.reshape((4, 2) + chunks.shape[1:])
    plane = pairs[:, 0] + swap(pairs[:, 1].astype(BF16), "dp", 1).astype(F32)
    diagonal = plane[3].astype(BF16)
    to_second = swap(diagonal[:half], "dp", 2).astype(F32)
    to_first = swap(diagonal[half:], "dp", 4).astype(F32)
    second = jnp.concatenate([plane[2, :half] + to_second, plane[2, half:]])
    first = jnp.concatenate([plane[1, :half], plane[1, half:] + to_first])
    total = plane[0] + swap(first.astype(BF16), "dp", 2).astype(F32)
    total = total + swap(second.astype(BF16), "dp", 4).astype(F32)
    low, high = total[:half].astype(BF16), total[half:].astype(BF16)
    low_other, high_other = swap(low, "seq", 1), swap(high, "seq", 3)
    low = (low.astype(F32) + low_other.astype(F32)).astype(BF16)
    high = (high.astype(F32) + high_other.astype(F32)).astype(BF16)
    low_other, high_other = swap(low, "seq", 3), swap(high, "seq", 1)
    return jnp.concatenate(
        [low.astype(F32) + low_other.astype(F32), high.astype(F32) + high_other.astype(F32)]
    )


def route(which):
    size, ring = lax.axis_size("dp"), lax.axis_size("seq")
    pairs = []
    for index in range(size):
        for place in range(ring):
            to_dp = (index & ~1) | (place >> 1)
            to_seq = 2 * ((place & 1) ^ which) + (index & 1)
            pairs.append((index * ring + place, to_dp * ring + to_seq))
    return pairs


def to_chip(slabs, place):
    parts = []
    for which in range(2):
        slab = lax.dynamic_index_in_dim(slabs, (place & 1) ^ which, 0, False)
        parts.append(lax.ppermute(slab, BOTH, route(which)))
    return jnp.concatenate(parts)


def from_chip(rows, place):
    half = rows.shape[0] // 2
    parts = []
    for which in range(2):
        back = [(target, source) for source, target in route(which)]
        parts.append(lax.ppermute(rows[which * half : (which + 1) * half], BOTH, back))
    parts = jnp.stack(parts)
    return jnp.where((place & 1) == 0, parts, parts[::-1])


def body(
    block_input,
    cotangent,
    segments,
    rand_blocks,
    w_attn,
    w_out,
    w_up,
    w_down,
    up_bias,
    bias_rows,
    norm_gains,
):
    micro, _, quarter, width = block_input.shape
    ring, size = lax.axis_size("seq"), lax.axis_size("dp")
    assert ring == 2 * micro and block_input.shape[1] == 1 and size % GROUP == 0
    heads, nblocks = rand_blocks.shape[:2]
    length = segments.shape[2]
    block = length // nblocks
    rows = 2 * quarter
    head = width // heads
    scale = head ** (-0.5)
    own, place = lax.axis_index("dp"), lax.axis_index("seq")
    core = own & 1

    tokens = to_chip(block_input[:, 0], place)
    upstream = to_chip(cotangent[:, 0], place).astype(F32)
    seg_own = segments[:, 0]
    seg_other = swap(seg_own, "dp", 1)
    seg = jnp.where((place & 1) == core, seg_own, seg_other)
    seg = lax.dynamic_index_in_dim(seg, place >> 1, 0, False).reshape(ring, quarter)
    per = quarter // block
    flip = place >> 1
    quarters = [2 * core + flip, 2 * core + 1 - flip, 2 * (1 - core) + flip, 2 * (1 - core) + 1 - flip]
    pick = lambda table, axis, wanted: jnp.concatenate(
        [lax.dynamic_index_in_dim(table, item, axis, False) for item in wanted], axis
    )
    key_blocks = jnp.concatenate([item * per + jnp.arange(per, dtype=jnp.int32) for item in quarters])
    query_blocks = key_blocks[: nblocks // 2]
    seg_key = pick(seg, 0, quarters)
    seg_query = seg_key[:rows]
    rand_query = pick(rand_blocks.reshape(heads, ring, per, -1), 1, quarters[:2])
    q_id, k_id = query_blocks[:, None], key_blocks[None]
    always = (jnp.abs(q_id - k_id) <= 1) | (q_id == 0) | (q_id == nblocks - 1) | (k_id == 0) | (k_id == nblocks - 1)
    hit = jnp.any(rand_query[:, :, :, None] == key_blocks[None, None, None, :], axis=2)
    seen = always[None] | hit
    seen = jnp.broadcast_to(
        seen[:, :, None, :, None], (heads, nblocks // 2, block, nblocks, block)
    ).reshape(heads, rows, length)
    allowed = seen & (seg_query[:, None] == seg_key[None, :])[None]

    part = width // size
    wide = w_up.shape[1]
    pack = lambda member: member.astype(BF16).reshape(part, -1, width).swapaxes(0, 1).reshape(-1, width)
    small = jnp.concatenate([bias_rows.reshape(-1), norm_gains.reshape(-1), up_bias])
    smalls = small.shape[0]
    small_rows = -(-smalls // (16 * width)) * 16
    small = jnp.pad(small, (0, small_rows * width - smalls)).astype(BF16).reshape(small_rows, width)
    n_attn, n_up, n_down = 3 * part, wide // width * part, wide // size
    group_one = by_owner(gather_chunks(jnp.concatenate([pack(w_attn), small])))
    group_two = by_owner(
        gather_chunks(jnp.concatenate([w_out.astype(BF16), pack(w_up), w_down.astype(BF16)]))
    )
    unpack = lambda chunks: chunks.reshape(size, -1, part, width).swapaxes(1, 2).reshape(size * part, -1)
    w_attn_b = unpack(group_one[:, :n_attn])
    flat = group_one[:, n_attn:].reshape(size, -1).astype(F32)
    bias_f = flat[:, : 6 * part].reshape(size, 6, part).swapaxes(0, 1).reshape(6, width)
    gain_f = flat[:, 6 * part : 8 * part].reshape(size, 2, part).swapaxes(0, 1).reshape(2, width)
    up_bias_f = flat[:, 8 * part : 8 * part + wide // size].reshape(-1)
    w_out_b = group_two[:, :part].reshape(width, width)
    w_up_b = unpack(group_two[:, part : part + n_up])
    w_down_b = group_two[:, part + n_up :].reshape(wide, width)

    projected = jnp.dot(tokens, w_attn_b, preferred_element_type=F32)
    queries = (projected[:, :width] + bias_f[0]).astype(BF16)
    keys = projected[:, width : 2 * width].astype(BF16)
    values = (projected[:, 2 * width :] + bias_f[1]).astype(BF16)
    pair = jnp.stack([keys, values])
    pair = jnp.concatenate([pair, swap(pair, "dp", 1)], axis=1)
    query_heads = queries.reshape(rows, heads, head)
    key_heads = pair[0].reshape(length, heads, head)
    value_heads = pair[1].reshape(length, heads, head)
    scores = jnp.einsum("qhd,khd->hqk", query_heads, key_heads, preferred_element_type=F32) * scale
    scores = jnp.where(allowed, scores, MASKED)
    row_max = jnp.max(scores, axis=-1, keepdims=True)
    exponent = jnp.exp(scores - row_max)
    row_total = jnp.sum(exponent, axis=-1, keepdims=True)
    attn_probs = exponent / row_total
    log_total = row_max + jnp.log(row_total)
    mixture = jnp.einsum("hqk,khd->qhd", attn_probs.astype(BF16), value_heads, preferred_element_type=F32)
    attended = mixture.reshape(rows, width).astype(BF16)
    branch = jnp.dot(attended, w_out_b, preferred_element_type=F32) + bias_f[2]
    first_norm, first_back = jax.vjp(layer_norm, tokens.astype(F32) + branch, gain_f[0], bias_f[4])
    first_low = first_norm.astype(BF16)
    pre_act = jnp.dot(first_low, w_up_b, preferred_element_type=F32) + up_bias_f
    act_float, gelu_back = jax.vjp(gelu_exact, pre_act)
    activation = act_float.astype(BF16)
    ffn_out = jnp.dot(activation, w_down_b, preferred_element_type=F32) + bias_f[3]
    result, second_back = jax.vjp(layer_norm, first_norm + ffn_out, gain_f[1], bias_f[5])
    output = from_chip(result.astype(BF16), place)

    grad_second, grad_gain_two, grad_shift_two = second_back(upstream)
    ffn_grad = grad_second.astype(BF16)
    grad_down = outer_grad(activation, ffn_grad)
    act_grad = times_transposed(ffn_grad, w_down_b)
    (pre_float,) = gelu_back(act_grad)
    pre_grad = pre_float.astype(BF16)
    grad_up = outer_grad(first_low, pre_grad)
    pack_up = lambda grad: grad.reshape(size, part, -1, width).swapaxes(1, 2).reshape(size, -1, width)
    sum_two = reduce_chunks(
        by_owner(jnp.concatenate([pack_up(grad_up), grad_down.reshape(size, -1, width)], axis=1))
    )

    first_grad = grad_second + times_transposed(pre_grad, w_up_b)
    grad_first, grad_gain_one, grad_shift_one = first_back(first_grad)
    branch_grad = grad_first.astype(BF16)
    grad_out = outer_grad(attended, branch_grad)
    attended_grad = times_transposed(branch_grad, w_out_b).astype(BF16).reshape(rows, heads, head)
    attn_probs = jnp.exp(scores - log_total)
    prob_grad = jnp.einsum("qhd,khd->hqk", attended_grad, value_heads, preferred_element_type=F32)
    row_dot = jnp.sum(prob_grad * attn_probs, axis=-1, keepdims=True)
    score_grad = (attn_probs * (prob_grad - row_dot)).astype(BF16)
    query_low = (
        jnp.einsum("hqk,khd->qhd", score_grad, key_heads, preferred_element_type=F32) * scale
    ).astype(BF16).reshape(rows, width)
    value_part = jnp.einsum("hqk,qhd->khd", attn_probs.astype(BF16), attended_grad, preferred_element_type=F32)
    key_part = jnp.einsum("hqk,qhd->khd", score_grad, query_heads, preferred_element_type=F32) * scale
    parts = jnp.stack([key_part.reshape(length, width), value_part.reshape(length, width)])
    parts = (parts[:, :rows] + swap(parts[:, rows:].astype(BF16), "dp", 1).astype(F32)).astype(BF16)
    key_low, value_low = parts[0], parts[1]
    proj_grad = jnp.concatenate([query_low, key_low, value_low], axis=1)
    grad_attn = outer_grad(tokens, proj_grad)
    input_grad = grad_first + times_transposed(proj_grad, w_attn_b)
    input_grad = from_chip(input_grad.astype(BF16), place).astype(F32)
    grad_biases = jnp.stack(
        [
            col_sums(query_low),
            col_sums(value_low),
            col_sums(branch_grad),
            col_sums(ffn_grad),
            grad_shift_one,
            grad_shift_two,
            grad_gain_one,
            grad_gain_two,
        ]
    )
    small_grad = jnp.concatenate(
        [
            grad_biases.reshape(8, size, part).swapaxes(0, 1).reshape(size, -1),
            col_sums(pre_grad).reshape(size, -1),
        ],
        axis=1,
    )
    small_grad = jnp.pad(small_grad, ((0, 0), (0, small_rows * width - smalls)))
    sum_one = reduce_chunks(
        by_owner(
            jnp.concatenate(
                [
                    pack_up(grad_attn),
                    grad_out.reshape(size, part, width),
                    small_grad.reshape(size, small_rows, width),
                ],
                axis=1,
            )
        )
    )
    unpack_own = lambda total: total.reshape(-1, part, width).swapaxes(0, 1).reshape(part, -1)
    small_sum = sum_one[n_attn + part :].reshape(-1)
    return (
        output[:, None],
        input_grad[:, None],
        unpack_own(sum_one[:n_attn]),
        sum_one[n_attn : n_attn + part],
        unpack_own(sum_two[:n_up]),
        sum_two[n_up:],
        small_sum[8 * part : 8 * part + wide // size],
        small_sum[: 6 * part].reshape(6, part),
        small_sum[6 * part : 8 * part].reshape(2, part),
    )


def solution(mesh):
    return jax.shard_map(
        body,
        mesh=mesh,
        in_specs=(
            P(None, "dp", "seq", None),
            P(None, "dp", "seq", None),
            P(None, "dp", None),
            P(),
            P("dp", None),
            P("dp", None),
            P("dp", None),
            P("dp", None),
            P("dp"),
            P(None, "dp"),
            P(None, "dp"),
        ),
        out_specs=(
            P(None, "dp", "seq", None),
            P(None, "dp", "seq", None),
            P("dp", None),
            P("dp", None),
            P("dp", None),
            P("dp", None),
            P("dp"),
            P(None, "dp"),
            P(None, "dp"),
        ),
        check_vma=False,
    )
```

```python
import jax
import jax.numpy as jnp
from jax import lax
from jax.experimental import pallas as pl
from jax.experimental.pallas import tpu as pltpu
from jax.sharding import PartitionSpec as P

EPSILON = 1e-05
HIDDEN = -1e30
LANES = 128
CHUNKS = 8
SMALL = 16
VMEM_BYTES = 56 * 1024 * 1024
BOTH = ("dp", "seq")
F32 = jnp.float32
BF16 = jnp.bfloat16
ANY = pl.BlockSpec(memory_space=pl.ANY)
SCALAR = pl.BlockSpec(memory_space=pltpu.SMEM)


def swap(value, axis, bit):
    size = lax.axis_size(axis)
    return lax.ppermute(value, axis, [(i, i ^ bit) for i in range(size)])


def halves(rows):
    return rows // 32 * 16


def gather_pieces(mine, fine):
    half = halves(mine.shape[0])
    first = swap(mine, "dp", 2 * fine)
    second = swap(mine, "dp", 4 * fine)
    low = swap(first[:half], "dp", 4 * fine)
    high = swap(second[half:], "dp", 2 * fine)
    even = (mine, first, second, low, high)
    return even + tuple(swap(piece, "dp", fine) for piece in even)


def reduce_chunks(keep, send, fine):
    add = lambda *terms: sum(term.astype(F32) for term in terms)
    rows = keep.shape[1]
    half = halves(rows)
    other = swap(send, "dp", fine)
    low = add(keep[3, :half], other[3, :half]).astype(BF16)
    high = add(keep[3, half:], other[3, half:]).astype(BF16)
    low = swap(low, "dp", 2 * fine)
    high = swap(high, "dp", 4 * fine)
    first = add(keep[1], other[1], jnp.pad(high, ((half, 0), (0, 0)))).astype(BF16)
    second = add(keep[2], other[2], jnp.pad(low, ((0, rows - half), (0, 0)))).astype(BF16)
    first = swap(first, "dp", 2 * fine)
    second = swap(second, "dp", 4 * fine)
    low = add(keep[0, :half], other[0, :half], first[:half], second[:half]).astype(BF16)
    high = add(keep[0, half:], other[0, half:], first[half:], second[half:]).astype(BF16)
    low = add(low, swap(low, "seq", 1)).astype(BF16)
    high = add(high, swap(high, "seq", 3)).astype(BF16)
    low = add(low, swap(low, "seq", 3))
    high = add(high, swap(high, "seq", 1))
    return low, high


def route(which):
    size, ring = lax.axis_size("dp"), lax.axis_size("seq")
    pairs = []
    for index in range(size):
        for place in range(ring):
            to_dp = (index & ~1) | (place >> 1)
            to_seq = 2 * ((place & 1) ^ which) + (index & 1)
            pairs.append((index * ring + place, to_dp * ring + to_seq))
    return pairs


def to_chip(slabs, place):
    parts = []
    for which in range(2):
        slab = lax.dynamic_index_in_dim(slabs, (place & 1) ^ which, 0, False)
        parts.append(lax.ppermute(slab, BOTH, route(which)))
    return parts


def from_chip(parts, place):
    back = []
    for which in range(2):
        pairs = [(target, source) for source, target in route(which)]
        back.append(lax.ppermute(parts[which], BOTH, pairs))
    back = jnp.stack(back)
    return jnp.where((place & 1) == 0, back, back[::-1])


def tn(left, right):
    return lax.dot_general(left, right, (((0,), (0,)), ((), ())), preferred_element_type=F32)


def nt(left, right):
    return lax.dot_general(left, right, (((1,), (1,)), ((), ())), preferred_element_type=F32)


def nn(left, right):
    return jnp.dot(left, right, preferred_element_type=F32)


def in_half(shape, which):
    lane = lax.broadcasted_iota(jnp.int32, shape, len(shape) - 1)
    return lane < LANES // 2 if which == 0 else lane >= LANES // 2


def attend_kernel(q_ref, own_ref, other_ref, q_mark_ref, k_mark_ref, out_ref, lse_ref):
    head = LANES // 2
    keys = jnp.concatenate([own_ref[0], other_ref[0]])
    values_t = jnp.concatenate([own_ref[1], other_ref[1]]).T
    mixed = []
    for e in range(2):
        k_side = jnp.where(in_half(keys.shape, e), keys, k_mark_ref[...])
        q_side = jnp.where(in_half(q_ref.shape, e), q_ref[...], q_mark_ref[e])
        scores = nt(k_side, q_side)
        top = jnp.max(scores, axis=0, keepdims=True)
        exponent = jnp.exp(scores - top)
        total = jnp.sum(exponent, axis=0, keepdims=True)
        part = nn(values_t[e * head : (e + 1) * head], exponent.astype(BF16))
        mixed.append(part * (1.0 / total))
        lse_ref[e : e + 1] = top + jnp.log(total)
    out_ref[...] = jnp.concatenate(mixed).T.astype(BF16)


def attend(q, own, other, q_mark, k_mark):
    rows, width = q.shape
    pairs = width // LANES
    length = k_mark.shape[0]
    heads = 2 * pairs
    kv_spec = pl.BlockSpec((2, rows, LANES), lambda j: (0, 0, j))
    return pl.pallas_call(
        attend_kernel,
        grid=(pairs,),
        in_specs=[
            pl.BlockSpec((rows, LANES), lambda j: (0, j)),
            kv_spec,
            kv_spec,
            pl.BlockSpec((2, rows, LANES), lambda j: (j, 0, 0)),
            pl.BlockSpec((length, LANES), lambda j: (0, 0)),
        ],
        out_specs=[
            pl.BlockSpec((rows, LANES), lambda j: (0, j)),
            pl.BlockSpec((None, 2, rows), lambda j: (j, 0, 0)),
        ],
        out_shape=[
            jax.ShapeDtypeStruct((rows, width), BF16),
            jax.ShapeDtypeStruct((pairs, 2, rows), F32),
        ],
        compiler_params=pltpu.CompilerParams(vmem_limit_bytes=VMEM_BYTES),
        cost_estimate=pl.CostEstimate(
            flops=4 * rows * length * LANES * heads,
            bytes_accessed=16 * rows * width,
            transcendentals=rows * length * heads,
        ),
        name="attend",
    )(q, own, other, q_mark, k_mark)


def attend_back_kernel(
    q_ref, own_ref, other_ref, q_mark_ref, k_mark_ref, out_ref, grad_ref, lse_ref, dq_ref, keep_ref, send_ref
):
    head = LANES // 2
    rows = q_ref.shape[0]
    keys = jnp.concatenate([own_ref[0], other_ref[0]])
    values = jnp.concatenate([own_ref[1], other_ref[1]])
    keys_t = keys.T
    grad = grad_ref[...]
    product = (out_ref[...].astype(F32) * grad.astype(F32)).T
    none = jnp.zeros_like(grad)
    dq, dk, dv = [], None, None
    for e in range(2):
        mine = in_half(keys.shape, e)
        mine_q = in_half(q_ref.shape, e)
        k_side = jnp.where(mine, keys, k_mark_ref[...])
        q_side = jnp.where(mine_q, q_ref[...], q_mark_ref[e])
        probs = jnp.exp(nt(k_side, q_side) - lse_ref[e : e + 1])
        prob_grad = nt(jnp.where(mine, values, jnp.zeros_like(values)), grad)
        row_dot = jnp.sum(product[e * head : (e + 1) * head], axis=0, keepdims=True)
        score_grad = (probs * (prob_grad - row_dot)).astype(BF16)
        dq.append(nn(keys_t[e * head : (e + 1) * head], score_grad))
        one_k = nn(score_grad, jnp.where(mine_q, q_ref[...], none))
        one_v = nn(probs.astype(BF16), jnp.where(mine_q, grad, none))
        dk = one_k if dk is None else dk + one_k
        dv = one_v if dv is None else dv + one_v
    dq_ref[...] = (jnp.concatenate(dq).T * head ** (-0.5)).astype(BF16)
    keep_ref[0] = dk[:rows]
    keep_ref[1] = dv[:rows]
    send_ref[0] = dk[rows:].astype(BF16)
    send_ref[1] = dv[rows:].astype(BF16)


def attend_back(q, own, other, q_mark, k_mark, out, grad, lse):
    rows, width = q.shape
    pairs = width // LANES
    length = k_mark.shape[0]
    heads = 2 * pairs
    row_spec = pl.BlockSpec((rows, LANES), lambda j: (0, j))
    kv_spec = pl.BlockSpec((2, rows, LANES), lambda j: (0, 0, j))
    return pl.pallas_call(
        attend_back_kernel,
        grid=(pairs,),
        in_specs=[
            row_spec,
            kv_spec,
            kv_spec,
            pl.BlockSpec((2, rows, LANES), lambda j: (j, 0, 0)),
            pl.BlockSpec((length, LANES), lambda j: (0, 0)),
            row_spec,
            row_spec,
            pl.BlockSpec((None, 2, rows), lambda j: (j, 0, 0)),
        ],
        out_specs=[row_spec, kv_spec, kv_spec],
        out_shape=[
            jax.ShapeDtypeStruct((rows, width), BF16),
            jax.ShapeDtypeStruct((2, rows, width), F32),
            jax.ShapeDtypeStruct((2, rows, width), BF16),
        ],
        compiler_params=pltpu.CompilerParams(vmem_limit_bytes=VMEM_BYTES),
        cost_estimate=pl.CostEstimate(
            flops=10 * rows * length * LANES * heads,
            bytes_accessed=32 * rows * width,
            transcendentals=rows * length * heads,
        ),
        name="attend_back",
    )(q, own, other, q_mark, k_mark, out, grad, lse)


def chunk_parts(pieces, rows):
    half = halves(rows)
    parts = {}
    for parity in range(2):
        mine, first, second, low, high = pieces[5 * parity : 5 * parity + 5]
        parts[parity] = [(mine, 0, rows)]
        parts[2 + parity] = [(first, 0, rows)]
        parts[4 + parity] = [(second, 0, rows)]
        parts[6 + parity] = [(low, 0, half), (high, half, rows)]
    return parts


def fetch(own, parts, start, size, target, sems):
    copies = []
    for k in range(CHUNKS):
        index = jnp.bitwise_xor(own, k)
        for ref, low, high in parts[k]:
            a, b = max(low, start), min(high, start + size)
            if a < b:
                into = target.at[pl.ds(pl.multiple_of(index * size + (a - start), 16), b - a)]
                copy = pltpu.make_async_copy(ref.at[pl.ds(a - low, b - a)], into, sems.at[len(copies)])
                copy.start()
                copies.append(copy)
    return copies


def wait_all(copies):
    for copy in copies:
        copy.wait()


def spread(own, source, part, keep, send, start, sems):
    copies = []
    for k in range(CHUNKS):
        rows = pl.ds(pl.multiple_of(jnp.bitwise_xor(own, k) * part, 16), part)
        into = (send if k % 2 else keep).at[k // 2, pl.ds(start, part)]
        copy = pltpu.make_async_copy(source.at[rows], into, sems.at[k])
        copy.start()
        copies.append(copy)
    return copies


def normalize(value):
    centre = value - jnp.mean(value, axis=-1, keepdims=True)
    rate = lax.rsqrt(jnp.mean(centre * centre, axis=-1, keepdims=True) + EPSILON)
    return centre * rate, rate


def normalize_back(grad, unit, rate):
    return rate * (
        grad - jnp.mean(grad, axis=-1, keepdims=True) - unit * jnp.mean(grad * unit, axis=-1, keepdims=True)
    )


def total_rows(value):
    return jnp.sum(value.astype(F32), axis=0, keepdims=True)


def kernel_params():
    return pltpu.CompilerParams(vmem_limit_bytes=VMEM_BYTES)


def key_value_kernel(part, own_ref, x0_ref, x1_ref, *refs):
    pieces, (kv_ref, small_ref, w_ref, tile_ref, sems) = refs[:10], refs[10:]
    rows = pieces[0].shape[0]
    parts = chunk_parts(pieces, rows)
    own = own_ref[0]
    tiles = fetch(own, parts, 3 * part, SMALL, tile_ref, sems.at[0])
    loads = [fetch(own, parts, (1 + i) * part, part, w_ref.at[i], sems.at[1 + i]) for i in range(2)]
    wait_all(tiles)
    small = sum(tile_ref[pl.ds(SMALL * k, SMALL)].astype(F32) for k in range(CHUNKS))
    small_ref[...] = small
    half = x0_ref.shape[0]
    for i in range(2):
        wait_all(loads[i])
        for h, x_ref in enumerate((x0_ref, x1_ref)):
            value = nn(x_ref[...], w_ref[i])
            if i == 1:
                value = value + small[1:2]
            kv_ref[i, pl.ds(h * half, half)] = value.astype(BF16)


def key_value(own, x0, x1, pieces):
    half, width = x0.shape
    part = width // CHUNKS
    return pl.pallas_call(
        lambda *refs: key_value_kernel(part, *refs),
        in_specs=[SCALAR, pl.BlockSpec(), pl.BlockSpec()] + [ANY] * 10,
        out_shape=[
            jax.ShapeDtypeStruct((2, 2 * half, width), BF16),
            jax.ShapeDtypeStruct((SMALL, width), F32),
        ],
        scratch_shapes=[
            pltpu.VMEM((2, width, width), BF16),
            pltpu.VMEM((CHUNKS * SMALL, width), BF16),
            pltpu.SemaphoreType.DMA((3, CHUNKS + 2)),
        ],
        compiler_params=kernel_params(),
        cost_estimate=pl.CostEstimate(
            flops=8 * half * width * width, bytes_accessed=8 * width * width, transcendentals=0
        ),
        name="key_value",
    )(own, x0, x1, *pieces)


def query_kernel(part, scale, own_ref, x0_ref, x1_ref, small_ref, *refs):
    pieces, (q_ref, w_ref, sems) = refs[:10], refs[10:]
    parts = chunk_parts(pieces, pieces[0].shape[0])
    wait_all(fetch(own_ref[0], parts, 0, part, w_ref, sems))
    half = x0_ref.shape[0]
    for h, x_ref in enumerate((x0_ref, x1_ref)):
        value = (nn(x_ref[...], w_ref[...]) + small_ref[0:1]).astype(BF16)
        q_ref[pl.ds(h * half, half)] = (value.astype(F32) * scale).astype(BF16)


def query(own, x0, x1, small, pieces, scale):
    half, width = x0.shape
    part = width // CHUNKS
    return pl.pallas_call(
        lambda *refs: query_kernel(part, scale, *refs),
        in_specs=[SCALAR] + [pl.BlockSpec()] * 3 + [ANY] * 10,
        out_shape=jax.ShapeDtypeStruct((2 * half, width), BF16),
        scratch_shapes=[pltpu.VMEM((width, width), BF16), pltpu.SemaphoreType.DMA((CHUNKS + 2,))],
        compiler_params=kernel_params(),
        cost_estimate=pl.CostEstimate(
            flops=4 * half * width * width, bytes_accessed=4 * width * width, transcendentals=0
        ),
        name="query",
    )(own, x0, x1, small, *pieces)


def up_kernel(part, own_ref, att_ref, x0_ref, x1_ref, small_ref, *refs):
    pieces, (unit_ref, rate_ref, act_ref, slope_ref, w_out, w_up, low_ref, sems) = refs[:10], refs[10:]
    parts = chunk_parts(pieces, pieces[0].shape[0])
    own = own_ref[0]
    blocks = w_up.shape[0]
    width = w_out.shape[1]
    loads = [fetch(own, parts, 0, part, w_out, sems.at[0])]
    for b in range(blocks):
        loads.append(fetch(own, parts, (1 + b) * part, part, w_up.at[b], sems.at[1 + b]))
    half = x0_ref.shape[0]
    wait_all(loads[0])
    for h, x_ref in enumerate((x0_ref, x1_ref)):
        rows = pl.ds(h * half, half)
        value = x_ref[...].astype(F32) + (nn(att_ref[rows], w_out[...]) + small_ref[2:3])
        unit, rate = normalize(value)
        unit_ref[rows] = unit
        rate_ref[rows] = jnp.broadcast_to(rate, (half, LANES))
        low_ref[rows] = (unit * small_ref[6:7] + small_ref[4:5]).astype(BF16)
    for b in range(blocks):
        wait_all(loads[1 + b])
        for h in range(2):
            rows, columns = pl.ds(h * half, half), pl.ds(b * width, width)
            pre = nn(low_ref[rows], w_up[b]) + small_ref[8 + b : 9 + b]
            chance = 0.5 + 0.5 * lax.erf(pre * 0.5**0.5)
            act_ref[rows, columns] = (pre * chance).astype(BF16)
            density = jnp.exp(-0.5 * pre * pre) * (0.5 / jnp.pi) ** 0.5
            slope_ref[rows, columns] = (chance + pre * density).astype(BF16)


def up(own, attended, x0, x1, small, pieces, wide):
    half, width = x0.shape
    rows, part, blocks = 2 * half, width // CHUNKS, wide // width
    return pl.pallas_call(
        lambda *refs: up_kernel(part, *refs),
        in_specs=[SCALAR] + [pl.BlockSpec()] * 4 + [ANY] * 10,
        out_shape=[
            jax.ShapeDtypeStruct((rows, width), F32),
            jax.ShapeDtypeStruct((rows, LANES), F32),
            jax.ShapeDtypeStruct((rows, wide), BF16),
            jax.ShapeDtypeStruct((rows, wide), BF16),
        ],
        scratch_shapes=[
            pltpu.VMEM((width, width), BF16),
            pltpu.VMEM((blocks, width, width), BF16),
            pltpu.VMEM((rows, width), BF16),
            pltpu.SemaphoreType.DMA((1 + blocks, CHUNKS + 2)),
        ],
        compiler_params=kernel_params(),
        cost_estimate=pl.CostEstimate(
            flops=2 * rows * width * (width + wide), bytes_accessed=2 * width * (width + wide), transcendentals=rows * wide
        ),
        name="up",
    )(own, attended, x0, x1, small, *pieces)


def down_kernel(part, own_ref, act_ref, slope_ref, unit_ref, rate_ref, c0_ref, c1_ref, small_ref, *refs):
    pieces_two, pieces_three = refs[:10], refs[10:20]
    out0_ref, out1_ref, first_ref, att_grad_ref, keep, send, sums_ref = refs[20:27]
    w_out, w_up, w_down, second_ref, ffn_low, first_low, back_ref, stage_up, stage_down, load_sems, store_sems = refs[27:]
    own = own_ref[0]
    blocks, width = w_up.shape[0], w_out.shape[1]
    wide = w_down.shape[0]
    deep = wide // CHUNKS
    parts = chunk_parts(pieces_three, deep)
    down_load = fetch(own, parts, 0, deep, w_down, load_sems.at[0])
    parts = chunk_parts(pieces_two, (1 + blocks) * part)
    up_load = [fetch(own, parts, (1 + b) * part, part, w_up.at[b], load_sems.at[1 + b]) for b in range(blocks)]
    out_load = fetch(own, parts, 0, part, w_out, load_sems.at[1 + blocks])
    half = c0_ref.shape[0]
    sums_ref[...] = jnp.zeros_like(sums_ref)
    wait_all(down_load)
    for h, (c_ref, o_ref) in enumerate(((c0_ref, out0_ref), (c1_ref, out1_ref))):
        rows = pl.ds(h * half, half)
        first = unit_ref[rows] * small_ref[6:7] + small_ref[4:5]
        first_low[rows] = first.astype(BF16)
        unit, rate = normalize(first + (nn(act_ref[rows], w_down[...]) + small_ref[3:4]))
        o_ref[...] = (unit * small_ref[7:8] + small_ref[5:6]).astype(BF16)
        grad = c_ref[...].astype(F32)
        second = normalize_back(grad * small_ref[7:8], unit, rate)
        low = second.astype(BF16)
        second_ref[rows] = second
        ffn_low[rows] = low
        sums_ref[3:4] += total_rows(low)
        sums_ref[5:6] += total_rows(grad)
        sums_ref[7:8] += total_rows(grad * unit)
    stores = [[], []]
    for load in up_load:
        wait_all(load)
    for i in range(blocks):
        b = jnp.bitwise_xor(own // 2, i)
        columns = pl.ds(pl.multiple_of(b * width, LANES), width)
        slot = i % 2
        w_block = w_down[pl.ds(pl.multiple_of(b * width, 16), width)]
        act_grad = nt(ffn_low[...], w_block)
        pre_grad = (act_grad * slope_ref[:, columns].astype(F32)).astype(BF16)
        sums_ref[pl.ds(8 + b, 1)] = total_rows(pre_grad)
        wait_all(stores[slot])
        stage_down[slot] = tn(act_ref[:, columns], ffn_low[...]).astype(BF16)
        stage_up[slot] = tn(first_low[...], pre_grad).astype(BF16)
        stores[slot] = spread(own, stage_up.at[slot], part, keep, send, b * part, store_sems.at[slot])
        for parity in range(2):
            rows = pl.ds(pl.multiple_of(jnp.bitwise_xor(own % 2, parity) * deep, 16), deep)
            into = (send if parity else keep).at[i, pl.ds(blocks * part, deep)]
            copy = pltpu.make_async_copy(stage_down.at[slot, rows], into, store_sems.at[slot, CHUNKS + parity])
            copy.start()
            stores[slot].append(copy)
        passed = nt(pre_grad, w_up[b])
        back_ref[...] = passed if i == 0 else back_ref[...] + passed
    wait_all(out_load)
    for h in range(2):
        rows = pl.ds(h * half, half)
        grad = second_ref[rows] + back_ref[rows]
        unit = unit_ref[rows]
        first = normalize_back(grad * small_ref[6:7], unit, rate_ref[rows][:, :1])
        low = first.astype(BF16)
        first_ref[rows] = first
        sums_ref[2:3] += total_rows(low)
        sums_ref[4:5] += total_rows(grad)
        sums_ref[6:7] += total_rows(grad * unit)
        att_grad_ref[rows] = nt(low, w_out[...]).astype(BF16)
    wait_all(stores[0])
    wait_all(stores[1])


def down(own, act, slope, unit, rate, c0, c1, small, pieces_two, pieces_three):
    half, width = c0.shape
    rows, wide = act.shape
    part, blocks = width // CHUNKS, wide // width
    chunk = jax.ShapeDtypeStruct((CHUNKS // 2, blocks * part + wide // CHUNKS, width), BF16)
    whole = pl.BlockSpec()
    return pl.pallas_call(
        lambda *refs: down_kernel(part, *refs),
        in_specs=[SCALAR] + [whole] * 7 + [ANY] * 20,
        out_specs=[whole] * 4 + [ANY, ANY, whole],
        out_shape=[
            jax.ShapeDtypeStruct((half, width), BF16),
            jax.ShapeDtypeStruct((half, width), BF16),
            jax.ShapeDtypeStruct((rows, width), F32),
            jax.ShapeDtypeStruct((rows, width), BF16),
            chunk,
            chunk,
            jax.ShapeDtypeStruct((SMALL, width), F32),
        ],
        scratch_shapes=[
            pltpu.VMEM((width, width), BF16),
            pltpu.VMEM((blocks, width, width), BF16),
            pltpu.VMEM((wide, width), BF16),
            pltpu.VMEM((rows, width), F32),
            pltpu.VMEM((rows, width), BF16),
            pltpu.VMEM((rows, width), BF16),
            pltpu.VMEM((rows, width), F32),
            pltpu.VMEM((2, width, width), BF16),
            pltpu.VMEM((2, width, width), BF16),
            pltpu.SemaphoreType.DMA((2 + blocks, CHUNKS + 2)),
            pltpu.SemaphoreType.DMA((2, CHUNKS + 2)),
        ],
        compiler_params=kernel_params(),
        cost_estimate=pl.CostEstimate(
            flops=2 * rows * width * (width + 5 * wide), bytes_accessed=20 * width * wide, transcendentals=0
        ),
        name="down",
    )(own, act, slope, unit, rate, c0, c1, small, *pieces_two, *pieces_three)


def query_back_kernel(part, own_ref, x0_ref, x1_ref, dq_ref, att_ref, first_ref, *refs):
    pieces = refs[:10]
    grad_ref, keep, send, sum_ref, w_ref, stage, load_sems, store_sems = refs[10:]
    own = own_ref[0]
    parts = chunk_parts(pieces, pieces[0].shape[0])
    load = fetch(own, parts, 0, part, w_ref, load_sems)
    half = x0_ref.shape[0]
    top, bottom = dq_ref[pl.ds(0, half)], dq_ref[pl.ds(half, half)]
    stage[0] = tn(att_ref[...], first_ref[...].astype(BF16)).astype(BF16)
    stores = spread(own, stage.at[0], part, keep, send, 0, store_sems.at[0])
    stage[1] = (tn(x0_ref[...], top) + tn(x1_ref[...], bottom)).astype(BF16)
    stores += spread(own, stage.at[1], part, keep, send, part, store_sems.at[1])
    sum_ref[...] = jnp.broadcast_to(total_rows(dq_ref[...]), sum_ref.shape)
    wait_all(load)
    grad_ref[...] = first_ref[...] + nt(dq_ref[...], w_ref[...])
    wait_all(stores)


def query_back(own, x0, x1, dq, attended, first, pieces):
    half, width = x0.shape
    rows, part = 2 * half, width // CHUNKS
    chunk = jax.ShapeDtypeStruct((CHUNKS // 2, 2 * part, width), BF16)
    whole = pl.BlockSpec()
    return pl.pallas_call(
        lambda *refs: query_back_kernel(part, *refs),
        in_specs=[SCALAR] + [whole] * 5 + [ANY] * 10,
        out_specs=[whole, ANY, ANY, whole],
        out_shape=[
            jax.ShapeDtypeStruct((rows, width), F32),
            chunk,
            chunk,
            jax.ShapeDtypeStruct((8, width), F32),
        ],
        scratch_shapes=[
            pltpu.VMEM((width, width), BF16),
            pltpu.VMEM((2, width, width), BF16),
            pltpu.SemaphoreType.DMA((CHUNKS + 2,)),
            pltpu.SemaphoreType.DMA((2, CHUNKS)),
        ],
        compiler_params=kernel_params(),
        cost_estimate=pl.CostEstimate(
            flops=6 * rows * width * width, bytes_accessed=12 * width * width, transcendentals=0
        ),
        name="query_back",
    )(own, x0, x1, dq, attended, first, *pieces)


def key_value_back_kernel(part, own_ref, x0_ref, x1_ref, kept_ref, came_ref, grad_ref, sum_ref, sums_ref, *refs):
    pieces = refs[:10]
    in0_ref, in1_ref, keep, send, w_ref, stage, tile_ref, load_sems, store_sems = refs[10:]
    own = own_ref[0]
    parts = chunk_parts(pieces, pieces[0].shape[0])
    loads = [fetch(own, parts, (1 + i) * part, part, w_ref.at[i], load_sems.at[i]) for i in range(2)]
    half = x0_ref.shape[0]
    stores = []
    low = []
    for i in range(2):
        value = (kept_ref[i] + came_ref[i].astype(F32)).astype(BF16)
        low.append(value)
        stage[i] = (tn(x0_ref[...], value[:half]) + tn(x1_ref[...], value[half:])).astype(BF16)
        stores += spread(own, stage.at[i], part, keep, send, i * part, store_sems.at[i])
    row = lax.broadcasted_iota(jnp.int32, sums_ref.shape, 0)
    sums = jnp.where(row == 0, sum_ref[0:1], sums_ref[...])
    tile_ref[...] = jnp.where(row == 1, total_rows(low[1]), sums).astype(BF16)
    for k in range(CHUNKS):
        into = (send if k % 2 else keep).at[k // 2, pl.ds(2 * part, SMALL)]
        copy = pltpu.make_async_copy(tile_ref, into, store_sems.at[2, k])
        copy.start()
        stores.append(copy)
    for load in loads:
        wait_all(load)
    for h, in_ref in enumerate((in0_ref, in1_ref)):
        rows = slice(h * half, (h + 1) * half)
        value = grad_ref[rows] + nt(low[0][rows], w_ref[0]) + nt(low[1][rows], w_ref[1])
        in_ref[...] = value.astype(BF16)
    wait_all(stores)


def key_value_back(own, x0, x1, kept, came, grad, query_sum, sums, pieces):
    half, width = x0.shape
    rows, part = 2 * half, width // CHUNKS
    chunk = jax.ShapeDtypeStruct((CHUNKS // 2, 2 * part + SMALL, width), BF16)
    whole = pl.BlockSpec()
    return pl.pallas_call(
        lambda *refs: key_value_back_kernel(part, *refs),
        in_specs=[SCALAR] + [whole] * 7 + [ANY] * 10,
        out_specs=[whole, whole, ANY, ANY],
        out_shape=[
            jax.ShapeDtypeStruct((half, width), BF16),
            jax.ShapeDtypeStruct((half, width), BF16),
            chunk,
            chunk,
        ],
        scratch_shapes=[
            pltpu.VMEM((2, width, width), BF16),
            pltpu.VMEM((2, width, width), BF16),
            pltpu.VMEM((SMALL, width), BF16),
            pltpu.SemaphoreType.DMA((2, CHUNKS + 2)),
            pltpu.SemaphoreType.DMA((3, CHUNKS)),
        ],
        compiler_params=kernel_params(),
        cost_estimate=pl.CostEstimate(
            flops=8 * rows * width * width, bytes_accessed=16 * width * width, transcendentals=0
        ),
        name="key_value_back",
    )(own, x0, x1, kept, came, grad, query_sum, sums, *pieces)


def body(
    block_input,
    cotangent,
    segments,
    rand_blocks,
    w_attn,
    w_out,
    w_up,
    w_down,
    up_bias,
    bias_rows,
    norm_gains,
):
    micro, _, quarter, width = block_input.shape
    ring, size = lax.axis_size("seq"), lax.axis_size("dp")
    assert ring == 2 * micro and block_input.shape[1] == 1 and size % CHUNKS == 0
    fine = size // CHUNKS
    groups = [[c * fine + i for i in range(fine)] for c in range(CHUNKS)]
    heads, nblocks = rand_blocks.shape[:2]
    length = segments.shape[2]
    block = length // nblocks
    rows = 2 * quarter
    head = width // heads
    device, place = lax.axis_index("dp"), lax.axis_index("seq")
    core = device & 1
    own = (device // fine).astype(jnp.int32).reshape(1)
    part, wide = width // CHUNKS, w_up.shape[1]

    tile = jnp.concatenate(
        [
            lax.dynamic_update_slice_in_dim(
                jnp.zeros((8, width), F32), jnp.concatenate([bias_rows, norm_gains]), device * (width // size), 1
            ),
            lax.dynamic_update_slice_in_dim(jnp.zeros((wide,), F32), up_bias, device * (wide // size), 0).reshape(
                wide // width, width
            ),
            jnp.zeros((SMALL - 8 - wide // width, width), F32),
        ]
    ).astype(BF16)
    shards = [member.astype(BF16) for member in (w_attn, w_out, w_up, w_down)]
    if fine > 1:
        shards = [lax.all_gather(member, "dp", axis_index_groups=groups, tiled=True) for member in shards]
        tile = jnp.sum(lax.all_gather(tile, "dp", axis_index_groups=groups).astype(F32), axis=0).astype(BF16)
    blocks_of = lambda member: [member[:, i : i + width] for i in range(0, member.shape[1], width)]
    x0, x1 = to_chip(block_input[:, 0], place)
    pieces_one = gather_pieces(jnp.concatenate(blocks_of(shards[0]) + [tile]), fine)
    pieces_two = gather_pieces(jnp.concatenate([shards[1]] + blocks_of(shards[2])), fine)
    pieces_three = gather_pieces(shards[3], fine)
    c0, c1 = to_chip(cotangent[:, 0], place)

    seg_own = segments[:, 0]
    seg_other = swap(seg_own, "dp", 1)
    seg = jnp.where((place & 1) == core, seg_own, seg_other)
    seg = lax.dynamic_index_in_dim(seg, place >> 1, 0, False).reshape(ring, quarter)
    per = quarter // block
    flip = place >> 1
    quarters = [2 * core + flip, 2 * core + 1 - flip, 2 * (1 - core) + flip, 2 * (1 - core) + 1 - flip]
    pick = lambda table, axis, wanted: jnp.concatenate(
        [lax.dynamic_index_in_dim(table, item, axis, False) for item in wanted], axis
    )
    key_blocks = jnp.concatenate([item * per + jnp.arange(per, dtype=jnp.int32) for item in quarters])
    query_blocks = key_blocks[: nblocks // 2]
    seg_key = pick(seg, 0, quarters)
    seg_query = seg_key[:rows]
    rand_query = pick(rand_blocks.reshape(heads, ring, per, -1), 1, quarters[:2])
    q_id, k_id = query_blocks[:, None], key_blocks[None]
    always = (jnp.abs(q_id - k_id) <= 1) | (q_id == 0) | (q_id == nblocks - 1) | (k_id == 0) | (k_id == nblocks - 1)
    hit = jnp.any(rand_query[:, :, :, None] == key_blocks[None, None, None, :], axis=2)
    seen = always[None] | hit
    lanes = LANES // 2
    kinds = jnp.arange(4, dtype=jnp.int32)
    q_table = jnp.broadcast_to(
        jnp.where(seen, 0.0, HIDDEN).astype(BF16)[:, :, None], (heads, nblocks // 2, block, nblocks)
    ).reshape(heads, rows, nblocks)
    q_segs = jnp.where(seg_query[:, None] == kinds[None], 0.0, HIDDEN).astype(BF16)
    q_mark = jnp.concatenate([q_table, jnp.broadcast_to(q_segs[None], (heads, rows, 4))], axis=2)
    q_mark = jnp.pad(q_mark, ((0, 0), (0, 0), (0, lanes - nblocks - 4)))
    q_mark = jnp.concatenate([q_mark, q_mark], axis=2)
    place_of = jnp.arange(length, dtype=jnp.int32)[:, None] // block
    k_mark = jnp.concatenate(
        [place_of == jnp.arange(nblocks, dtype=jnp.int32)[None], seg_key[:, None] == kinds[None]], axis=1
    ).astype(BF16)
    k_mark = jnp.pad(k_mark, ((0, 0), (0, lanes - nblocks - 4)))
    k_mark = jnp.concatenate([k_mark, k_mark], axis=1)

    own_kv, small = key_value(own, x0, x1, pieces_one)
    other_kv = swap(own_kv, "dp", 1)
    queries = query(own, x0, x1, small, pieces_one, head ** (-0.5))
    attended, log_total = attend(queries, own_kv, other_kv, q_mark, k_mark)
    unit, rate, act, slope = up(own, attended, x0, x1, small, pieces_two, wide)
    out0, out1, first, att_grad, keep_ffn, send_ffn, sums = down(
        own, act, slope, unit, rate, c0, c1, small, pieces_two, pieces_three
    )
    output = from_chip((out0, out1), place)
    ffn_sum = reduce_chunks(keep_ffn, send_ffn, fine)
    query_grad, kept, sent = attend_back(
        queries, own_kv, other_kv, q_mark, k_mark, attended, att_grad, log_total
    )
    came = swap(sent, "dp", 1)
    input_part, keep_one, send_one, query_sum = query_back(own, x0, x1, query_grad, attended, first, pieces_one)
    one_sum = reduce_chunks(keep_one, send_one, fine)
    in0, in1, keep_two, send_two = key_value_back(
        own, x0, x1, kept, came, input_part, query_sum, sums, pieces_one
    )
    two_sum = reduce_chunks(keep_two, send_two, fine)
    input_grad = from_chip((in0, in1), place).astype(F32)

    def blocks_at(halves_sum, start, count, span):
        value = jnp.concatenate(halves_sum)
        members = [value[start + i * span : start + (i + 1) * span] for i in range(count)]
        return members[0] if count == 1 else jnp.concatenate(members, axis=1)

    grads = [
        jnp.concatenate([blocks_at(one_sum, part, 1, part), blocks_at(two_sum, 0, 2, part)], axis=1),
        blocks_at(one_sum, 0, 1, part),
        blocks_at(ffn_sum, 0, wide // width, part),
        blocks_at(ffn_sum, wide // width * part, 1, wide // CHUNKS),
    ]
    tile = blocks_at(two_sum, 2 * part, 1, SMALL)
    if fine > 1:
        grads = [
            lax.psum_scatter(member, "dp", scatter_dimension=0, axis_index_groups=groups, tiled=True)
            for member in grads
        ]
        tile = lax.psum(tile, "dp", axis_index_groups=groups)
    rows_own = lax.dynamic_slice_in_dim(tile[:8], device * (width // size), width // size, 1)
    up_own = lax.dynamic_slice_in_dim(tile[8 : 8 + wide // width].reshape(-1), device * (wide // size), wide // size, 0)
    return (output[:, None], input_grad[:, None], *grads, up_own, rows_own[:6], rows_own[6:8])


def solution(mesh):
    return jax.shard_map(
        body,
        mesh=mesh,
        in_specs=(
            P(None, "dp", "seq", None),
            P(None, "dp", "seq", None),
            P(None, "dp", None),
            P(),
            P("dp", None),
            P("dp", None),
            P("dp", None),
            P("dp", None),
            P("dp"),
            P(None, "dp"),
            P(None, "dp"),
        ),
        out_specs=(
            P(None, "dp", "seq", None),
            P(None, "dp", "seq", None),
            P("dp", None),
            P("dp", None),
            P("dp", None),
            P("dp", None),
            P("dp"),
            P(None, "dp"),
            P(None, "dp"),
        ),
        check_vma=False,
    )
```
